128 devices in a mesh: blk: 16 (over x_hi, z, core), tile: 8 (over x_lo, y).
Axes of the slice: x: 4 (x_hi: 2, x_lo: 2; x = x_hi * 2 + x_lo), y: 4, z: 4, core: 2. Of those that a mesh axis runs over, the one named last changes fastest.
Arguments:
- features: bfloat16 [8192, 8192], P('tile', 'blk'), may hold values from -6 to 6
- weight_kv: bfloat16 [8192, 12288], P(None, 'blk'), may hold values from -0.0625 to 0.0625
- key_gain: float32 [6, 128], replicated, may hold values from 0.1 to 1.9
- block_reader: int32 [64], P('tile'), may hold values from 0 to 7, as said below
Outputs:
- routed_kv: bfloat16 [32768, 12288], P('tile', 'blk')
The draws below stay inside these ranges and needn't reach their ends.
Inputs may be any that keep to these rules, and one draw needn't show every extreme that they name: `block_reader`: at most 4 of the 8 blocks of one index of tile name the same reader, and one reader is named by exactly 4 blocks of every index of tile.
All inputs are finite; a program needn't handle non-finite values.
Results may differ from the reference program's by a relative error of at most 0.001.
Values may be sent and summed in bfloat16 or wider, within the bound.
A program may use at most 192 MiB of HBM per device.

```python
import jax
import jax.numpy as jnp
from jax import lax

D = 8192
KVH = 8
HD = 128
L = 6
BT = 128
BPS = 8
CAP = 4
TOKENS = 8192
BLOCKS = 64
SLOTS = 256
KVALL = 12288


def draw_block_reader(key, part):
    sources = BLOCKS // BPS
    key_heavy, key_others, key_order = jax.random.split(key, 3)
    heaviest = jax.random.randint(key_heavy, (), 0, sources)
    others_part = jax.random.randint(key_others, (sources, BPS - CAP), 0, sources - 1)
    others_part = others_part + (others_part >= heaviest).astype(jnp.int32)
    stacked = jnp.concatenate([jnp.full((sources, CAP), heaviest, jnp.int32), others_part.astype(jnp.int32)], axis=1)
    orders = jax.vmap(lambda row_key: jax.random.permutation(row_key, BPS))(jax.random.split(key_order, sources))
    return jnp.take_along_axis(stacked, orders, axis=1).reshape(BLOCKS).astype(jnp.int32)


def block_scale(own_key, dims, cuts, low, largest):
    def one(dim, shards_of):
        heights = jax.random.uniform(jax.random.fold_in(jax.random.fold_in(own_key, 6), dim), (shards_of,), jnp.float32, low / len(cuts), largest / len(cuts))
        return jnp.repeat(jnp.exp(heights), dims[dim] // shards_of).reshape((-1,) + (1,) * (len(dims) - dim - 1))

    level = one(*cuts[0])
    for cut in cuts[1:]:
        level = level * one(*cut)
    return level


def noise(key, shape, scale, reach, cuts=(), kind=jnp.bfloat16):
    result = scale * jax.random.normal(key, shape, jnp.float32)
    if cuts:
        result = result * block_scale(key, shape, cuts, -0.22, 0.18)
    return jnp.clip(result, -reach, reach).astype(kind)


def setup_inputs(seed: int = 0) -> dict:
    seeds = jax.random.split(jax.random.key(seed), 5)
    return {
        "features": noise(seeds[0], (TOKENS, D), 1.0, 6.0, ((0, 8), (1, 16))),
        "weight_kv": noise(seeds[1], (D, KVALL), D ** -0.5, 0.0625, ((1, 16),)),
        "key_gain": jnp.clip(1.0 + 0.18 * jax.random.normal(seeds[2], (L, HD), jnp.float32), 0.1, 1.9),
        "block_reader": draw_block_reader(jax.random.fold_in(seeds[4], 71), 0),
    }


norm_eps = 1e-05

def reference(features, weight_kv, key_gain, block_reader):
    pieces = []
    layer_cols = 2 * KVH * HD
    for layer_id in range(L):
        w_rows = weight_kv[:, layer_id * layer_cols:(layer_id + 1) * layer_cols]
        projected = jnp.dot(features, w_rows, preferred_element_type=jnp.float32).reshape(-1, KVH, 2, HD)
        key_part = projected[:, :, 0]
        mean_square = lax.optimization_barrier(jnp.mean(key_part * key_part, axis=-1, keepdims=True))
        key_part = key_part * lax.rsqrt(mean_square + norm_eps) * key_gain[layer_id][None, None, :]
        joined = jnp.stack([key_part, projected[:, :, 1]], axis=2).reshape(-1, layer_cols)
        pieces.append(joined.astype(jnp.bfloat16))
    key_value = jnp.concatenate(pieces, axis=1)
    sources = BLOCKS // BPS
    onehot = (block_reader[:, None] == jnp.arange(sources, dtype=jnp.int32)[None, :]).astype(jnp.int32)
    onehot = onehot.reshape(sources, BPS, sources)
    earlier = jnp.cumsum(onehot, axis=1) - onehot
    slot_rank = lax.optimization_barrier(jnp.sum(earlier * onehot, axis=2)).reshape(BLOCKS).astype(jnp.int32)
    source = (jnp.arange(BLOCKS, dtype=jnp.int32) // BPS).astype(jnp.int32)
    target = ((block_reader * sources + source) * CAP + slot_rank).astype(jnp.int32)
    routed = jnp.zeros((SLOTS, BT, KVALL), jnp.bfloat16)
    routed = routed.at[target].set(key_value.reshape(BLOCKS, BT, KVALL))
    return routed.reshape(SLOTS * BT, KVALL)
```

```python
import jax
import jax.numpy as jnp
from jax import lax
from jax.experimental import pallas as pl
from jax.experimental.pallas import tpu as pltpu
from jax.sharding import PartitionSpec as P

KVH = 8
HD = 128
BT = 128
BPS = 8
CAP = 4
Q = 8
HALF = 64
ROWS = 2 * HALF
PIECE = 512
WIDTH = 8192
COLS = 768
PAIRS = 3

norm_eps = 1e-05


def device(h, z, c, l, y):
    return {"blk": (h * 4 + z) * 2 + c, "tile": l * 4 + y}


def kv_kernel(x_ref, w_hbm, gain_ref, br_ref, cand_ref, meta_out, feats, w_ref, kv, near, pay_own, pay_near,
              meta_v, meta_s, link_send, link_recv, sib_recv, near_recv, y_send, y_recv, meta_send, meta_recv,
              local_sem, w_sem, smem_sem):
    b = lax.axis_index("blk")
    t = lax.axis_index("tile")
    h, z, c = b // 8, (b // 2) % 4, b % 2
    l, y = t // 4, t % 4
    zp, zm, z2 = (z + 1) % 4, (z + 3) % 4, (z + 2) % 4
    h2 = 1 - h
    other = (1 - l) * 4 + y

    w_copy = pltpu.make_async_copy(w_hbm, w_ref, w_sem)
    w_copy.start()

    barrier = pltpu.get_barrier_semaphore()
    friends = [device(h2, z, c, l, y), device(h, zp, c, l, y), device(h, zm, c, l, y), device(h, z, 1 - c, l, y)]
    peers = []
    for dl in range(2):
        for dy in range(4):
            if dl or dy:
                peers.append(device(h, z, c, (l + dl) % 2, (y + dy) % 4))
    for d in friends + peers:
        pl.semaphore_signal(barrier, inc=1, device_id=d, device_id_type=pl.DeviceIdType.MESH)

    br = [br_ref[k] for k in range(BPS)]
    heavy = jnp.int32(0)
    for r in reversed(range(8)):
        count = sum((br[k] == r).astype(jnp.int32) for k in range(BPS))
        heavy = jnp.where(count == CAP, jnp.int32(r), heavy)
    h_block = [jnp.int32(0)] * CAP
    r_block = [jnp.int32(0)] * CAP
    r_reader = [jnp.int32(0)] * CAP
    h_seen, r_seen = jnp.int32(0), jnp.int32(0)
    for k in range(BPS):
        is_h = (br[k] == heavy).astype(jnp.int32)
        for j in range(CAP):
            take_h = is_h * (h_seen == j).astype(jnp.int32)
            take_r = (1 - is_h) * (r_seen == j).astype(jnp.int32)
            h_block[j] = h_block[j] + take_h * k
            r_block[j] = r_block[j] + take_r * k
            r_reader[j] = r_reader[j] + take_r * br[k]
        h_seen = h_seen + is_h
        r_seen = r_seen + (1 - is_h)

    def cols(piece):
        return pl.ds(pl.multiple_of(piece * PIECE, PIECE), PIECE)

    for i in range(CAP):
        for half in range(2):
            q = 2 * i + half
            feats[q, 0:HALF, cols(b)] = x_ref[2 * h_block[i] + half]
            feats[q, HALF:ROWS, cols(b)] = x_ref[2 * r_block[i] + half]
    row = lax.broadcasted_iota(jnp.int32, (8, 128), 0)
    info = jnp.where(row == 4, heavy, 0)
    for j in range(CAP):
        info = jnp.where(row == j, r_reader[j], info)
    meta_v[t] = info

    pl.semaphore_wait(barrier, len(friends) + len(peers))

    def piece_of(ph, pz, pc):
        return (ph * 4 + pz) * 2 + pc

    def view(q, piece):
        return feats.at[q, :, cols(piece)]

    def remote(src, dst, ss, rs, d):
        return pltpu.make_async_remote_copy(src_ref=src, dst_ref=dst, send_sem=ss, recv_sem=rs, device_id=d,
                                            device_id_type=pl.DeviceIdType.MESH)

    to_h = device(h2, z, c, l, y)
    to_p = device(h, zp, c, l, y)
    to_m = device(h, zm, c, l, y)
    to_c = device(h, z, 1 - c, l, y)
    own = piece_of(h, z, c)
    got = [piece_of(h2, z, c), piece_of(h, zm, c), piece_of(h, zp, c), piece_of(h2, zm, c), piece_of(h2, zp, c),
           piece_of(h, z2, c), piece_of(h2, z2, c)]

    def link(q, piece, kind, d):
        remote(view(q, piece), view(q, piece), link_send.at[kind], link_recv.at[q, kind], d).start()

    def arrived(q, kind):
        v = view(q, got[kind])
        remote(v, v, link_send.at[kind], link_recv.at[q, kind], to_p).wait_recv()

    def sib(q, piece):
        remote(view(q, piece), view(q, piece), link_send.at[7], sib_recv.at[q], to_c).start()

    def begin(q):
        link(q, own, 0, to_h)
        link(q, own, 1, to_p)
        link(q, own, 2, to_m)
        sib(q, own)

    def y_dev(dy):
        return device(h, z, c, l, (y + dy) % 4)

    def spread(q, pay, which, source):
        for dy in (2, 1, 3):
            remote(pay.at[q, dy], cand_ref.at[source, q], y_send.at[which, dy], y_recv.at[which, dy], y_dev(dy)).start()
        pltpu.make_async_copy(pay.at[q, 0], cand_ref.at[source, q], local_sem.at[which]).start()

    begin(0)
    metas = []
    for i, d in enumerate(peers):
        dl, dy = (i + 1) // 4, (i + 1) % 4
        cp = remote(meta_v.at[t], meta_v.at[t], meta_send.at[i], meta_recv.at[i], d)
        cp.start()
        metas.append((dl, dy))

    def step(k, carry):
        @pl.when(k + 1 < Q)
        def _():
            begin(k + 1)

        @pl.when(k < Q)
        def _():
            arrived(k, 0)
            link(k, got[0], 3, to_p)
            link(k, got[0], 4, to_m)
            sib(k, got[0])
            arrived(k, 1)
            link(k, got[1], 5, to_p)
            sib(k, got[1])
            arrived(k, 4)
            link(k, got[4], 6, to_m)
            sib(k, got[4])

        @pl.when((k >= 1) & (k < Q + 1))
        def _():
            for kind in (2, 3, 5, 6):
                arrived(k - 1, kind)
                sib(k - 1, got[kind])

        @pl.when(k == 2)
        def _():
            w_copy.wait()
            for i, (dl, dy) in enumerate(metas):
                source = ((l + dl) % 2) * 4 + (y - dy + 4) % 4
                remote(meta_v.at[source], meta_v.at[source], meta_send.at[i], meta_recv.at[i], to_p).wait()
            to_s = pltpu.make_async_copy(meta_v, meta_s, smem_sem)
            to_s.start()
            to_s.wait()

        @pl.when((k >= 2) & (k < Q + 2))
        def _():
            q = k - 2
            both = feats.at[q, :, 0:WIDTH // 2]
            remote(both, both, link_send.at[7], sib_recv.at[q], to_c).wait_recv()
            for j in range(PAIRS):
                at = slice(j * 2 * HD, (j + 1) * 2 * HD)
                acc = jnp.dot(feats[q], w_ref[:, at], preferred_element_type=jnp.float32)
                key = acc[:, :HD]
                layer = (b * PAIRS + j) // KVH
                scale = lax.rsqrt(jnp.mean(key * key, axis=-1, keepdims=True) + norm_eps)
                key = key * scale * gain_ref[pl.ds(layer, 1), :]
                both_kv = jnp.concatenate([key, acc[:, HD:]], axis=1).astype(jnp.bfloat16)
                h_part, r_part = both_kv[:HALF], both_kv[HALF:]
                kv[q, 0, :, at] = h_part
                kv[q, 1, :, at] = r_part
                for dy in range(4):
                    mine = heavy == l * 4 + (y + dy) % 4
                    pay_own[q, dy, :, at] = jnp.where(mine, h_part, r_part)

        @pl.when((k >= 3) & (k < Q + 3))
        def _():
            q = k - 3
            remote(near.at[q], near.at[q], link_send.at[8], near_recv.at[q], to_p).wait_recv()
            near_heavy = meta_s[other, 4, 0]
            h_part, r_part = near[q, 0], near[q, 1]
            for dy in range(4):
                mine = near_heavy == l * 4 + (y + dy) % 4
                pay_near[q, dy] = jnp.where(mine, h_part, r_part)

        @pl.when((k >= 2) & (k < Q + 2))
        def _():
            q = k - 2
            remote(kv.at[q], near.at[q], link_send.at[8], near_recv.at[q], device(h, z, c, 1 - l, y)).start()
            spread(q, pay_own, 0, t)

        @pl.when((k >= 3) & (k < Q + 3))
        def _():
            spread(k - 3, pay_near, 1, other)

        return carry

    lax.fori_loop(0, Q + 3, step, 0)
    meta_out[...] = meta_v[...]

    one = feats.at[:, :, 0:PIECE]
    for kind in range(7):
        remote(one, one, link_send.at[kind], link_recv.at[0, kind], to_p).wait_send()
    eight = feats.at[:, :, 0:WIDTH // 2]
    remote(eight, eight, link_send.at[7], sib_recv.at[0], to_c).wait_send()
    remote(kv, near, link_send.at[8], near_recv.at[0], to_p).wait_send()
    for which, pay in ((0, pay_own), (1, pay_near)):
        for dy in (1, 2, 3):
            source = (l if which == 0 else 1 - l) * 4 + (y - dy + 4) % 4
            cp = remote(pay.at[:, dy], cand_ref.at[source], y_send.at[which, dy], y_recv.at[which, dy], to_p)
            cp.wait_send()
            cp.wait_recv()
        pltpu.make_async_copy(pay.at[:, 0], cand_ref.at[t if which == 0 else other], local_sem.at[which]).wait()


def place_kernel(meta_ref, cand_ref, out_ref):
    t = lax.axis_index("tile")
    is_h = (meta_ref[0, 4, 0] == t).astype(jnp.int32)
    pick = [is_h * c for c in range(CAP)]
    used = [is_h] * CAP
    seen = jnp.int32(0)
    for j in range(CAP):
        named = (1 - is_h) * (meta_ref[0, j, 0] == t).astype(jnp.int32)
        for c in range(CAP):
            hit = named * (seen == c).astype(jnp.int32)
            pick[c] = pick[c] + hit * j
            used[c] = used[c] + hit
        seen = seen + named
    for c in range(CAP):
        block = cand_ref[0, pick[c]]
        out_ref[0, c] = jnp.where(used[c] > 0, block, jnp.zeros_like(block))


def shards(features, weight_kv, key_gain, block_reader):
    dma = pltpu.SemaphoreType.DMA
    bf16 = jnp.bfloat16
    vmem = pl.BlockSpec(memory_space=pltpu.VMEM)
    hbm = pl.BlockSpec(memory_space=pl.ANY)
    cand, meta = pl.pallas_call(
        kv_kernel,
        out_shape=(
            jax.ShapeDtypeStruct((8, Q, HALF, COLS), bf16),
            jax.ShapeDtypeStruct((8, 8, 128), jnp.int32),
        ),
        in_specs=[vmem, hbm, vmem, pl.BlockSpec(memory_space=pltpu.SMEM)],
        out_specs=(hbm, vmem),
        scratch_shapes=[
            pltpu.VMEM((Q, ROWS, WIDTH), bf16),
            pltpu.VMEM((WIDTH, COLS), bf16),
            pltpu.VMEM((Q, 2, HALF, COLS), bf16),
            pltpu.VMEM((Q, 2, HALF, COLS), bf16),
            pltpu.VMEM((Q, 4, HALF, COLS), bf16),
            pltpu.VMEM((Q, 4, HALF, COLS), bf16),
            pltpu.VMEM((8, 8, 128), jnp.int32),
            pltpu.SMEM((8, 8, 128), jnp.int32),
            dma((9,)),
            dma((Q, 7)),
            dma((Q,)),
            dma((Q,)),
            dma((2, 4)),
            dma((2, 4)),
            dma((7,)),
            dma((7,)),
            dma((2,)),
            dma,
            dma,
        ],
        compiler_params=pltpu.CompilerParams(
            collective_id=0, has_side_effects=True, vmem_limit_bytes=60 * 2**20
        ),
        name="gather_project_route",
    )(features.reshape(16, HALF, PIECE), weight_kv, key_gain, block_reader)
    slots = pl.pallas_call(
        place_kernel,
        grid=(8,),
        out_shape=jax.ShapeDtypeStruct((8, CAP, BT, COLS), bf16),
        in_specs=[
            pl.BlockSpec((1, 8, 128), lambda s: (s, 0, 0), memory_space=pltpu.SMEM),
            pl.BlockSpec((1, CAP, BT, COLS), lambda s: (s, 0, 0, 0)),
        ],
        out_specs=pl.BlockSpec((1, CAP, BT, COLS), lambda s: (s, 0, 0, 0)),
        name="place_slots",
    )(meta, cand.reshape(8, CAP, BT, COLS))
    return slots.reshape(8 * CAP * BT, COLS)


def solution(mesh):
    return jax.shard_map(
        shards,
        mesh=mesh,
        in_specs=(P("tile", "blk"), P(None, "blk"), P(), P("tile")),
        out_specs=P("tile", "blk"),
        check_vma=False,
    )
```

```python
import jax
import jax.numpy as jnp
from jax import lax
from jax.experimental import pallas as pl
from jax.experimental.pallas import tpu as pltpu
from jax.sharding import PartitionSpec as P

KVH = 8
HD = 128
BT = 128
BPS = 8
CAP = 4
PARTS = 2
Q = CAP * PARTS
HALF = BT // PARTS
ROWS = 2 * HALF
PIECE = 512
PIECES = 16
WIDTH = 8192
COLS = 768
PAIRS = 3

norm_eps = 1e-05


def device(h, z, c, l, y):
    return {"blk": (h * 4 + z) * 2 + c, "tile": l * 4 + y}


def kv_kernel(x_ref, w_hbm, gain_ref, br_ref, cand_ref, meta_out, feats, w_ref, kv, near, pay_own, pay_near,
              meta_v, meta_s, link_send, link_recv, sib_recv, near_recv, y_send, y_recv, meta_send, meta_recv,
              local_sem, w_sem, smem_sem):
    b = lax.axis_index("blk")
    t = lax.axis_index("tile")
    h, z, c = b // 8, (b // 2) % 4, b % 2
    l, y = t // 4, t % 4
    zp, zm, z2 = (z + 1) % 4, (z + 3) % 4, (z + 2) % 4
    h2 = 1 - h
    other = (1 - l) * 4 + y

    w_copy = pltpu.make_async_copy(w_hbm, w_ref, w_sem)
    w_copy.start()

    barrier = pltpu.get_barrier_semaphore()
    friends = [device(h2, z, c, l, y), device(h, zp, c, l, y), device(h, zm, c, l, y), device(h, z, 1 - c, l, y)]
    peers = []
    for dl in range(2):
        for dy in range(4):
            if dl or dy:
                peers.append(device(h, z, c, (l + dl) % 2, (y + dy) % 4))
    for d in friends + peers:
        pl.semaphore_signal(barrier, inc=1, device_id=d, device_id_type=pl.DeviceIdType.MESH)

    br = [br_ref[k] for k in range(BPS)]
    heavy = jnp.int32(0)
    for r in reversed(range(8)):
        count = sum((br[k] == r).astype(jnp.int32) for k in range(BPS))
        heavy = jnp.where(count == CAP, jnp.int32(r), heavy)
    h_block = [jnp.int32(0)] * CAP
    r_block = [jnp.int32(0)] * CAP
    r_reader = [jnp.int32(0)] * CAP
    h_seen, r_seen = jnp.int32(0), jnp.int32(0)
    for k in range(BPS):
        is_h = (br[k] == heavy).astype(jnp.int32)
        for j in range(CAP):
            take_h = is_h * (h_seen == j).astype(jnp.int32)
            take_r = (1 - is_h) * (r_seen == j).astype(jnp.int32)
            h_block[j] = h_block[j] + take_h * k
            r_block[j] = r_block[j] + take_r * k
            r_reader[j] = r_reader[j] + take_r * br[k]
        h_seen = h_seen + is_h
        r_seen = r_seen + (1 - is_h)

    for i in range(CAP):
        for part in range(PARTS):
            q = PARTS * i + part
            feats[q, b, 0:HALF] = x_ref[PARTS * h_block[i] + part]
            feats[q, b, HALF:ROWS] = x_ref[PARTS * r_block[i] + part]
    row = lax.broadcasted_iota(jnp.int32, (8, 128), 0)
    info = jnp.where(row == 4, heavy, 0)
    for j in range(CAP):
        info = jnp.where(row == j, r_reader[j], info)
    meta_v[t] = info

    pl.semaphore_wait(barrier, len(friends) + len(peers))

    def piece_of(ph, pz, pc):
        return (ph * 4 + pz) * 2 + pc

    def view(q, piece):
        return feats.at[q, piece]

    def remote(src, dst, ss, rs, d):
        return pltpu.make_async_remote_copy(src_ref=src, dst_ref=dst, send_sem=ss, recv_sem=rs, device_id=d,
                                            device_id_type=pl.DeviceIdType.MESH)

    to_h = device(h2, z, c, l, y)
    to_p = device(h, zp, c, l, y)
    to_m = device(h, zm, c, l, y)
    to_c = device(h, z, 1 - c, l, y)
    own = piece_of(h, z, c)
    got = [piece_of(h2, z, c), piece_of(h, zm, c), piece_of(h, zp, c), piece_of(h2, zm, c), piece_of(h2, zp, c),
           piece_of(h, z2, c), piece_of(h2, z2, c)]

    def link(q, piece, kind, d):
        remote(view(q, piece), view(q, piece), link_send.at[kind], link_recv.at[q, kind], d).start()

    def arrived(q, kind):
        v = view(q, got[kind])
        remote(v, v, link_send.at[kind], link_recv.at[q, kind], to_p).wait_recv()

    def sib(q, piece):
        remote(view(q, piece), view(q, piece), link_send.at[7], sib_recv.at[q], to_c).start()

    def begin(q):
        link(q, own, 0, to_h)
        link(q, own, 1, to_p)
        link(q, own, 2, to_m)
        sib(q, own)

    def y_dev(dy):
        return device(h, z, c, l, (y + dy) % 4)

    def spread(q, pay, which, source):
        for dy in (2, 1, 3):
            remote(pay.at[q, dy], cand_ref.at[source, q], y_send.at[which, dy], y_recv.at[which, dy], y_dev(dy)).start()
        pltpu.make_async_copy(pay.at[q, 0], cand_ref.at[source, q], local_sem.at[which]).start()

    begin(0)
    metas = []
    for i, d in enumerate(peers):
        dl, dy = (i + 1) // 4, (i + 1) % 4
        cp = remote(meta_v.at[t], meta_v.at[t], meta_send.at[i], meta_recv.at[i], d)
        cp.start()
        metas.append((dl, dy))

    def step(k, carry):
        @pl.when(k + 1 < Q)
        def _():
            begin(k + 1)

        @pl.when(k < Q)
        def _():
            arrived(k, 0)
            link(k, got[0], 3, to_p)
            link(k, got[0], 4, to_m)
            sib(k, got[0])

        @pl.when((k >= 1) & (k < Q + 1))
        def _():
            arrived(k - 1, 4)
            link(k - 1, got[4], 6, to_m)
            sib(k - 1, got[4])

        @pl.when(k < Q)
        def _():
            arrived(k, 1)
            link(k, got[1], 5, to_p)
            sib(k, got[1])

        @pl.when((k >= 1) & (k < Q + 1))
        def _():
            for kind in (2, 3, 5):
                arrived(k - 1, kind)
                sib(k - 1, got[kind])

        @pl.when((k >= 2) & (k < Q + 2))
        def _():
            arrived(k - 2, 6)
            sib(k - 2, got[6])

        @pl.when(k == 2)
        def _():
            w_copy.wait()
            for i, (dl, dy) in enumerate(metas):
                source = ((l + dl) % 2) * 4 + (y - dy + 4) % 4
                remote(meta_v.at[source], meta_v.at[source], meta_send.at[i], meta_recv.at[i], to_p).wait()
            to_s = pltpu.make_async_copy(meta_v, meta_s, smem_sem)
            to_s.start()
            to_s.wait()

        @pl.when((k >= 2) & (k < Q + 2))
        def _():
            q = k - 2
            both = feats.at[q, 0:PIECES // 2]
            remote(both, both, link_send.at[7], sib_recv.at[q], to_c).wait_recv()
            for j in range(PAIRS):
                at = slice(j * 2 * HD, (j + 1) * 2 * HD)
                rows = jnp.concatenate([feats[q, p] for p in range(PIECES)], axis=1)
                acc = jnp.dot(rows, w_ref[:, at], preferred_element_type=jnp.float32)
                key = acc[:, :HD]
                layer = (b * PAIRS + j) // KVH
                scale = lax.rsqrt(jnp.mean(key * key, axis=-1, keepdims=True) + norm_eps)
                key = key * scale * gain_ref[pl.ds(layer, 1), :]
                both_kv = jnp.concatenate([key, acc[:, HD:]], axis=1).astype(jnp.bfloat16)
                h_part, r_part = both_kv[:HALF], both_kv[HALF:]
                kv[q, 0, :, at] = h_part
                kv[q, 1, :, at] = r_part
                for dy in range(4):
                    mine = heavy == l * 4 + (y + dy) % 4
                    pay_own[q, dy, :, at] = jnp.where(mine, h_part, r_part)

        @pl.when((k >= 3) & (k < Q + 3))
        def _():
            q = k - 3
            remote(near.at[q], near.at[q], link_send.at[8], near_recv.at[q], to_p).wait_recv()
            near_heavy = meta_s[other, 4, 0]
            h_part, r_part = near[q, 0], near[q, 1]
            for dy in range(4):
                mine = near_heavy == l * 4 + (y + dy) % 4
                pay_near[q, dy] = jnp.where(mine, h_part, r_part)

        @pl.when((k >= 2) & (k < Q + 2))
        def _():
            q = k - 2
            remote(kv.at[q], near.at[q], link_send.at[8], near_recv.at[q], device(h, z, c, 1 - l, y)).start()
            spread(q, pay_own, 0, t)

        @pl.when((k >= 3) & (k < Q + 3))
        def _():
            spread(k - 3, pay_near, 1, other)

        return carry

    lax.fori_loop(0, Q + 3, step, 0)
    meta_out[...] = meta_v[...]

    one = feats.at[:, 0]
    for kind in range(7):
        remote(one, one, link_send.at[kind], link_recv.at[0, kind], to_p).wait_send()
    eight = feats.at[:, 0:PIECES // 2]
    remote(eight, eight, link_send.at[7], sib_recv.at[0], to_c).wait_send()
    remote(kv, near, link_send.at[8], near_recv.at[0], to_p).wait_send()
    for which, pay in ((0, pay_own), (1, pay_near)):
        for dy in (1, 2, 3):
            source = (l if which == 0 else 1 - l) * 4 + (y - dy + 4) % 4
            cp = remote(pay.at[:, dy], cand_ref.at[source], y_send.at[which, dy], y_recv.at[which, dy], to_p)
            cp.wait_send()
            cp.wait_recv()
        pltpu.make_async_copy(pay.at[:, 0], cand_ref.at[t if which == 0 else other], local_sem.at[which]).wait()


def place_kernel(meta_ref, cand_ref, out_ref, took, made, read_sem, write_sem):
    t = lax.axis_index("tile")
    for s in range(8):
        pltpu.make_async_copy(cand_ref.at[s], took.at[s], read_sem.at[s]).start()

    def place(s, carry):
        is_h = (meta_ref[s, 4, 0] == t).astype(jnp.int32)
        pick = [is_h * c for c in range(CAP)]
        used = [is_h] * CAP
        seen = jnp.int32(0)
        for j in range(CAP):
            named = (1 - is_h) * (meta_ref[s, j, 0] == t).astype(jnp.int32)
            for c in range(CAP):
                hit = named * (seen == c).astype(jnp.int32)
                pick[c] = pick[c] + hit * j
                used[c] = used[c] + hit
            seen = seen + named
        pltpu.make_async_copy(cand_ref.at[s], took.at[s], read_sem.at[s]).wait()
        for c in range(CAP):
            block = took[s, pick[c]]
            made[s, c] = jnp.where(used[c] > 0, block, jnp.zeros_like(block))
        pltpu.make_async_copy(made.at[s], out_ref.at[s], write_sem.at[s]).start()
        return carry

    lax.fori_loop(0, 8, place, 0)
    for s in range(8):
        pltpu.make_async_copy(made.at[s], out_ref.at[s], write_sem.at[s]).wait()


def shards(features, weight_kv, key_gain, block_reader):
    dma = pltpu.SemaphoreType.DMA
    bf16 = jnp.bfloat16
    vmem = pl.BlockSpec(memory_space=pltpu.VMEM)
    hbm = pl.BlockSpec(memory_space=pl.ANY)
    cand, meta = pl.pallas_call(
        kv_kernel,
        out_shape=(
            jax.ShapeDtypeStruct((8, Q, HALF, COLS), bf16),
            jax.ShapeDtypeStruct((8, 8, 128), jnp.int32),
        ),
        in_specs=[vmem, hbm, vmem, pl.BlockSpec(memory_space=pltpu.SMEM)],
        out_specs=(hbm, vmem),
        scratch_shapes=[
            pltpu.VMEM((Q, PIECES, ROWS, PIECE), bf16),
            pltpu.VMEM((WIDTH, COLS), bf16),
            pltpu.VMEM((Q, 2, HALF, COLS), bf16),
            pltpu.VMEM((Q, 2, HALF, COLS), bf16),
            pltpu.VMEM((Q, 4, HALF, COLS), bf16),
            pltpu.VMEM((Q, 4, HALF, COLS), bf16),
            pltpu.VMEM((8, 8, 128), jnp.int32),
            pltpu.SMEM((8, 8, 128), jnp.int32),
            dma((9,)),
            dma((Q, 7)),
            dma((Q,)),
            dma((Q,)),
            dma((2, 4)),
            dma((2, 4)),
            dma((7,)),
            dma((7,)),
            dma((2,)),
            dma,
            dma,
        ],
        compiler_params=pltpu.CompilerParams(
            collective_id=0, has_side_effects=True, vmem_limit_bytes=60 * 2**20
        ),
        name="gather_project_route",
    )(features.reshape(BPS * PARTS, HALF, PIECE), weight_kv, key_gain, block_reader)
    slots = pl.pallas_call(
        place_kernel,
        out_shape=jax.ShapeDtypeStruct((8, CAP, BT, COLS), bf16),
        in_specs=[pl.BlockSpec(memory_space=pltpu.SMEM), hbm],
        out_specs=hbm,
        scratch_shapes=[
            pltpu.VMEM((8, CAP, BT, COLS), bf16),
            pltpu.VMEM((8, CAP, BT, COLS), bf16),
            dma((8,)),
            dma((8,)),
        ],
        name="place_slots",
    )(meta, cand.reshape(8, CAP, BT, COLS))
    return slots.reshape(8 * CAP * BT, COLS)


def solution(mesh):
    return jax.shard_map(
        shards,
        mesh=mesh,
        in_specs=(P("tile", "blk"), P(None, "blk"), P(), P("tile")),
        out_specs=P("tile", "blk"),
        check_vma=False,
    )
```

```python
import jax
import jax.numpy as jnp
from jax import lax
from jax.experimental import pallas as pl
from jax.experimental.pallas import tpu as pltpu
from jax.sharding import PartitionSpec as P

KVH = 8
HD = 128
BT = 128
BPS = 8
CAP = 4
PARTS = 4
Q = CAP * PARTS
HALF = BT // PARTS
ROWS = 2 * HALF
PIECE = 512
PIECES = 16
WIDTH = 8192
COLS = 768
PAIRS = 3

norm_eps = 1e-05


def device(h, z, c, l, y):
    return {"blk": (h * 4 + z) * 2 + c, "tile": l * 4 + y}


def kv_kernel(x_ref, w_hbm, gain_ref, br_ref, cand_ref, meta_out, feats, w_ref, kv, near, pay_own, pay_near,
              meta_v, meta_s, link_send, link_recv, sib_recv, near_recv, y_send, y_recv, meta_send, meta_recv,
              local_sem, w_sem, smem_sem):
    b = lax.axis_index("blk")
    t = lax.axis_index("tile")
    h, z, c = b // 8, (b // 2) % 4, b % 2
    l, y = t // 4, t % 4
    zp, zm, z2 = (z + 1) % 4, (z + 3) % 4, (z + 2) % 4
    h2 = 1 - h
    other = (1 - l) * 4 + y

    w_copy = pltpu.make_async_copy(w_hbm, w_ref, w_sem)
    w_copy.start()

    barrier = pltpu.get_barrier_semaphore()
    friends = [device(h2, z, c, l, y), device(h, zp, c, l, y), device(h, zm, c, l, y), device(h, z, 1 - c, l, y)]
    peers = []
    for dl in range(2):
        for dy in range(4):
            if dl or dy:
                peers.append(device(h, z, c, (l + dl) % 2, (y + dy) % 4))
    for d in friends + peers:
        pl.semaphore_signal(barrier, inc=1, device_id=d, device_id_type=pl.DeviceIdType.MESH)

    br = [br_ref[k] for k in range(BPS)]
    heavy = jnp.int32(0)
    for r in reversed(range(8)):
        count = sum((br[k] == r).astype(jnp.int32) for k in range(BPS))
        heavy = jnp.where(count == CAP, jnp.int32(r), heavy)
    h_block = [jnp.int32(0)] * CAP
    r_block = [jnp.int32(0)] * CAP
    r_reader = [jnp.int32(0)] * CAP
    h_seen, r_seen = jnp.int32(0), jnp.int32(0)
    for k in range(BPS):
        is_h = (br[k] == heavy).astype(jnp.int32)
        for j in range(CAP):
            take_h = is_h * (h_seen == j).astype(jnp.int32)
            take_r = (1 - is_h) * (r_seen == j).astype(jnp.int32)
            h_block[j] = h_block[j] + take_h * k
            r_block[j] = r_block[j] + take_r * k
            r_reader[j] = r_reader[j] + take_r * br[k]
        h_seen = h_seen + is_h
        r_seen = r_seen + (1 - is_h)

    for i in range(CAP):
        for part in range(PARTS):
            q = PARTS * i + part
            feats[q, b, 0:HALF] = x_ref[PARTS * h_block[i] + part]
            feats[q, b, HALF:ROWS] = x_ref[PARTS * r_block[i] + part]
    row = lax.broadcasted_iota(jnp.int32, (8, 128), 0)
    info = jnp.where(row == 4, heavy, 0)
    for j in range(CAP):
        info = jnp.where(row == j, r_reader[j], info)
    meta_v[t] = info

    pl.semaphore_wait(barrier, len(friends) + len(peers))

    def piece_of(ph, pz, pc):
        return (ph * 4 + pz) * 2 + pc

    def view(q, piece):
        return feats.at[q, piece]

    def remote(src, dst, ss, rs, d):
        return pltpu.make_async_remote_copy(src_ref=src, dst_ref=dst, send_sem=ss, recv_sem=rs, device_id=d,
                                            device_id_type=pl.DeviceIdType.MESH)

    to_h = device(h2, z, c, l, y)
    to_p = device(h, zp, c, l, y)
    to_m = device(h, zm, c, l, y)
    to_c = device(h, z, 1 - c, l, y)
    own = piece_of(h, z, c)
    got = [piece_of(h2, z, c), piece_of(h, zm, c), piece_of(h, zp, c), piece_of(h2, zm, c), piece_of(h2, zp, c),
           piece_of(h, z2, c), piece_of(h2, z2, c)]

    def link(q, piece, kind, d):
        remote(view(q, piece), view(q, piece), link_send.at[kind], link_recv.at[q, kind], d).start()

    def arrived(q, kind):
        v = view(q, got[kind])
        remote(v, v, link_send.at[kind], link_recv.at[q, kind], to_p).wait_recv()

    def sib(q, piece):
        remote(view(q, piece), view(q, piece), link_send.at[7], sib_recv.at[q], to_c).start()

    def begin(q):
        link(q, own, 0, to_h)
        link(q, own, 1, to_p)
        link(q, own, 2, to_m)
        sib(q, own)

    def y_dev(dy):
        return device(h, z, c, l, (y + dy) % 4)

    def spread(q, pay, which, source):
        for dy in (2, 1, 3):
            remote(pay.at[q, dy], cand_ref.at[source, q], y_send.at[which, dy], y_recv.at[which, dy], y_dev(dy)).start()
        pltpu.make_async_copy(pay.at[q, 0], cand_ref.at[source, q], local_sem.at[which]).start()

    for k in range(3):
        begin(k)
    metas = []
    for i, d in enumerate(peers):
        dl, dy = (i + 1) // 4, (i + 1) % 4
        cp = remote(meta_v.at[t], meta_v.at[t], meta_send.at[i], meta_recv.at[i], d)
        cp.start()
        metas.append((dl, dy))

    def step(k, carry):
        @pl.when(k + 3 < Q)
        def _():
            begin(k + 3)

        @pl.when(k < Q)
        def _():
            arrived(k, 0)
            link(k, got[0], 3, to_p)
            link(k, got[0], 4, to_m)
            sib(k, got[0])

        @pl.when((k >= 1) & (k < Q + 1))
        def _():
            arrived(k - 1, 4)
            link(k - 1, got[4], 6, to_m)
            sib(k - 1, got[4])

        @pl.when(k < Q)
        def _():
            arrived(k, 1)
            link(k, got[1], 5, to_p)
            sib(k, got[1])

        @pl.when((k >= 1) & (k < Q + 1))
        def _():
            for kind in (2, 3, 5):
                arrived(k - 1, kind)
                sib(k - 1, got[kind])

        @pl.when((k >= 2) & (k < Q + 2))
        def _():
            arrived(k - 2, 6)
            sib(k - 2, got[6])

        @pl.when(k == 2)
        def _():
            w_copy.wait()
            for i, (dl, dy) in enumerate(metas):
                source = ((l + dl) % 2) * 4 + (y - dy + 4) % 4
                remote(meta_v.at[source], meta_v.at[source], meta_send.at[i], meta_recv.at[i], to_p).wait()
            to_s = pltpu.make_async_copy(meta_v, meta_s, smem_sem)
            to_s.start()
            to_s.wait()

        @pl.when((k >= 3) & (k < Q + 3))
        def _():
            q = k - 3
            both = feats.at[q, 0:PIECES // 2]
            remote(both, both, link_send.at[7], sib_recv.at[q], to_c).wait_recv()
            for j in range(PAIRS):
                at = slice(j * 2 * HD, (j + 1) * 2 * HD)
                rows = jnp.concatenate([feats[q, p] for p in range(PIECES)], axis=1)
                acc = jnp.dot(rows, w_ref[:, at], preferred_element_type=jnp.float32)
                key = acc[:, :HD]
                layer = (b * PAIRS + j) // KVH
                scale = lax.rsqrt(jnp.mean(key * key, axis=-1, keepdims=True) + norm_eps)
                key = key * scale * gain_ref[pl.ds(layer, 1), :]
                both_kv = jnp.concatenate([key, acc[:, HD:]], axis=1).astype(jnp.bfloat16)
                h_part, r_part = both_kv[:HALF], both_kv[HALF:]
                kv[q, 0, :, at] = h_part
                kv[q, 1, :, at] = r_part
                for dy in range(4):
                    mine = heavy == l * 4 + (y + dy) % 4
                    pay_own[q, dy, :, at] = jnp.where(mine, h_part, r_part)

        @pl.when((k >= 4) & (k < Q + 4))
        def _():
            q = k - 4
            remote(near.at[q], near.at[q], link_send.at[8], near_recv.at[q], to_p).wait_recv()
            near_heavy = meta_s[other, 4, 0]
            h_part, r_part = near[q, 0], near[q, 1]
            for dy in range(4):
                mine = near_heavy == l * 4 + (y + dy) % 4
                pay_near[q, dy] = jnp.where(mine, h_part, r_part)

        @pl.when((k >= 3) & (k < Q + 3))
        def _():
            q = k - 3
            remote(kv.at[q], near.at[q], link_send.at[8], near_recv.at[q], device(h, z, c, 1 - l, y)).start()
            spread(q, pay_own, 0, t)

        @pl.when((k >= 4) & (k < Q + 4))
        def _():
            spread(k - 4, pay_near, 1, other)

        return carry

    lax.fori_loop(0, Q + 4, step, 0)
    meta_out[...] = meta_v[...]

    one = feats.at[:, 0]
    for kind in range(7):
        remote(one, one, link_send.at[kind], link_recv.at[0, kind], to_p).wait_send()
    eight = feats.at[:, 0:PIECES // 2]
    remote(eight, eight, link_send.at[7], sib_recv.at[0], to_c).wait_send()
    remote(kv, near, link_send.at[8], near_recv.at[0], to_p).wait_send()
    for which, pay in ((0, pay_own), (1, pay_near)):
        for dy in (1, 2, 3):
            source = (l if which == 0 else 1 - l) * 4 + (y - dy + 4) % 4
            cp = remote(pay.at[:, dy], cand_ref.at[source], y_send.at[which, dy], y_recv.at[which, dy], to_p)
            cp.wait_send()
            cp.wait_recv()
        pltpu.make_async_copy(pay.at[:, 0], cand_ref.at[t if which == 0 else other], local_sem.at[which]).wait()


def place_kernel(meta_ref, cand_ref, out_ref, took, made, read_sem, write_sem):
    t = lax.axis_index("tile")
    for s in range(8):
        pltpu.make_async_copy(cand_ref.at[s], took.at[s], read_sem.at[s]).start()

    def place(s, carry):
        is_h = (meta_ref[s, 4, 0] == t).astype(jnp.int32)
        pick = [is_h * c for c in range(CAP)]
        used = [is_h] * CAP
        seen = jnp.int32(0)
        for j in range(CAP):
            named = (1 - is_h) * (meta_ref[s, j, 0] == t).astype(jnp.int32)
            for c in range(CAP):
                hit = named * (seen == c).astype(jnp.int32)
                pick[c] = pick[c] + hit * j
                used[c] = used[c] + hit
            seen = seen + named
        pltpu.make_async_copy(cand_ref.at[s], took.at[s], read_sem.at[s]).wait()
        for c in range(CAP):
            block = took[s, pick[c]]
            made[s, c] = jnp.where(used[c] > 0, block, jnp.zeros_like(block))
        pltpu.make_async_copy(made.at[s], out_ref.at[s], write_sem.at[s]).start()
        return carry

    lax.fori_loop(0, 8, place, 0)
    for s in range(8):
        pltpu.make_async_copy(made.at[s], out_ref.at[s], write_sem.at[s]).wait()


def shards(features, weight_kv, key_gain, block_reader):
    dma = pltpu.SemaphoreType.DMA
    bf16 = jnp.bfloat16
    vmem = pl.BlockSpec(memory_space=pltpu.VMEM)
    hbm = pl.BlockSpec(memory_space=pl.ANY)
    cand, meta = pl.pallas_call(
        kv_kernel,
        out_shape=(
            jax.ShapeDtypeStruct((8, Q, HALF, COLS), bf16),
            jax.ShapeDtypeStruct((8, 8, 128), jnp.int32),
        ),
        in_specs=[vmem, hbm, vmem, pl.BlockSpec(memory_space=pltpu.SMEM)],
        out_specs=(hbm, vmem),
        scratch_shapes=[
            pltpu.VMEM((Q, PIECES, ROWS, PIECE), bf16),
            pltpu.VMEM((WIDTH, COLS), bf16),
            pltpu.VMEM((Q, 2, HALF, COLS), bf16),
            pltpu.VMEM((Q, 2, HALF, COLS), bf16),
            pltpu.VMEM((Q, 4, HALF, COLS), bf16),
            pltpu.VMEM((Q, 4, HALF, COLS), bf16),
            pltpu.VMEM((8, 8, 128), jnp.int32),
            pltpu.SMEM((8, 8, 128), jnp.int32),
            dma((9,)),
            dma((Q, 7)),
            dma((Q,)),
            dma((Q,)),
            dma((2, 4)),
            dma((2, 4)),
            dma((7,)),
            dma((7,)),
            dma((2,)),
            dma,
            dma,
        ],
        compiler_params=pltpu.CompilerParams(
            collective_id=0, has_side_effects=True, vmem_limit_bytes=60 * 2**20
        ),
        name="gather_project_route",
    )(features.reshape(BPS * PARTS, HALF, PIECE), weight_kv, key_gain, block_reader)
    slots = pl.pallas_call(
        place_kernel,
        out_shape=jax.ShapeDtypeStruct((8, CAP, BT, COLS), bf16),
        in_specs=[pl.BlockSpec(memory_space=pltpu.SMEM), hbm],
        out_specs=hbm,
        scratch_shapes=[
            pltpu.VMEM((8, CAP, BT, COLS), bf16),
            pltpu.VMEM((8, CAP, BT, COLS), bf16),
            dma((8,)),
            dma((8,)),
        ],
        name="place_slots",
    )(meta, cand.reshape(8, CAP, BT, COLS))
    return slots.reshape(8 * CAP * BT, COLS)


def solution(mesh):
    return jax.shard_map(
        shards,
        mesh=mesh,
        in_specs=(P("tile", "blk"), P(None, "blk"), P(), P("tile")),
        out_specs=P("tile", "blk"),
        check_vma=False,
    )
```

```python
import jax
import jax.numpy as jnp
from jax import lax
from jax.experimental import pallas as pl
from jax.experimental.pallas import tpu as pltpu
from jax.sharding import PartitionSpec as P

KVH = 8
HD = 128
BT = 128
BPS = 8
CAP = 4
PARTS = 4
Q = CAP * PARTS
HALF = BT // PARTS
ROWS = 2 * HALF
PIECE = 512
PIECES = 16
WIDTH = 8192
COLS = 768
PAIRS = 3

norm_eps = 1e-05


def device(h, z, c, l, y):
    return {"blk": (h * 4 + z) * 2 + c, "tile": l * 4 + y}


def kv_kernel(x_ref, w_hbm, gain_ref, br_ref, cand_ref, meta_out, feats, w_ref, kv, near, pay_own, pay_near,
              meta_v, meta_s, link_send, link_recv, sib_recv, near_recv, y_send, y_recv, meta_send, meta_recv,
              local_sem, w_sem, smem_sem):
    b = lax.axis_index("blk")
    t = lax.axis_index("tile")
    h, z, c = b // 8, (b // 2) % 4, b % 2
    l, y = t // 4, t % 4
    zp, zm, z2 = (z + 1) % 4, (z + 3) % 4, (z + 2) % 4
    h2 = 1 - h
    other = (1 - l) * 4 + y

    w_copy = pltpu.make_async_copy(w_hbm, w_ref, w_sem)
    w_copy.start()

    barrier = pltpu.get_barrier_semaphore()
    friends = [device(h2, z, c, l, y), device(h, zp, c, l, y), device(h, zm, c, l, y), device(h, z, 1 - c, l, y)]
    peers = []
    for dl in range(2):
        for dy in range(4):
            if dl or dy:
                peers.append(device(h, z, c, (l + dl) % 2, (y + dy) % 4))
    for d in friends + peers:
        pl.semaphore_signal(barrier, inc=1, device_id=d, device_id_type=pl.DeviceIdType.MESH)

    br = [br_ref[k] for k in range(BPS)]
    heavy = jnp.int32(0)
    for r in reversed(range(8)):
        count = sum((br[k] == r).astype(jnp.int32) for k in range(BPS))
        heavy = jnp.where(count == CAP, jnp.int32(r), heavy)
    h_block = [jnp.int32(0)] * CAP
    r_block = [jnp.int32(0)] * CAP
    r_reader = [jnp.int32(0)] * CAP
    h_seen, r_seen = jnp.int32(0), jnp.int32(0)
    for k in range(BPS):
        is_h = (br[k] == heavy).astype(jnp.int32)
        for j in range(CAP):
            take_h = is_h * (h_seen == j).astype(jnp.int32)
            take_r = (1 - is_h) * (r_seen == j).astype(jnp.int32)
            h_block[j] = h_block[j] + take_h * k
            r_block[j] = r_block[j] + take_r * k
            r_reader[j] = r_reader[j] + take_r * br[k]
        h_seen = h_seen + is_h
        r_seen = r_seen + (1 - is_h)

    for i in range(CAP):
        for part in range(PARTS):
            q = PARTS * i + part
            feats[q, b, 0:HALF] = x_ref[PARTS * h_block[i] + part]
            feats[q, b, HALF:ROWS] = x_ref[PARTS * r_block[i] + part]
    row = lax.broadcasted_iota(jnp.int32, (8, 128), 0)
    info = jnp.where(row == 4, heavy, 0)
    for j in range(CAP):
        info = jnp.where(row == j, r_reader[j], info)
    meta_v[t] = info

    pl.semaphore_wait(barrier, len(friends) + len(peers))

    def piece_of(ph, pz, pc):
        return (ph * 4 + pz) * 2 + pc

    def view(q, piece):
        return feats.at[q, piece]

    def remote(src, dst, ss, rs, d):
        return pltpu.make_async_remote_copy(src_ref=src, dst_ref=dst, send_sem=ss, recv_sem=rs, device_id=d,
                                            device_id_type=pl.DeviceIdType.MESH)

    to_h = device(h2, z, c, l, y)
    to_p = device(h, zp, c, l, y)
    to_m = device(h, zm, c, l, y)
    to_c = device(h, z, 1 - c, l, y)
    own = piece_of(h, z, c)
    got = [piece_of(h2, z, c), piece_of(h, zm, c), piece_of(h, zp, c), piece_of(h2, zm, c), piece_of(h2, zp, c),
           piece_of(h, z2, c), piece_of(h2, z2, c)]

    def link(q, piece, kind, d):
        remote(view(q, piece), view(q, piece), link_send.at[kind], link_recv.at[q, kind], d).start()

    def arrived(q, kind):
        v = view(q, got[kind])
        remote(v, v, link_send.at[kind], link_recv.at[q, kind], to_p).wait_recv()

    def sib(q, piece):
        remote(view(q, piece), view(q, piece), link_send.at[7], sib_recv.at[q], to_c).start()

    def begin(q):
        link(q, own, 0, to_h)
        link(q, own, 1, to_p)
        link(q, own, 2, to_m)
        sib(q, own)

    def y_dev(dy):
        return device(h, z, c, l, (y + dy) % 4)

    def spread(q, pay, which, source):
        for dy in (2, 1, 3):
            remote(pay.at[q, dy], cand_ref.at[source, q], y_send.at[which, dy], y_recv.at[which, dy], y_dev(dy)).start()
        pltpu.make_async_copy(pay.at[q, 0], cand_ref.at[source, q], local_sem.at[which]).start()

    for k in range(3):
        begin(k)
    metas = []
    for i, d in enumerate(peers):
        dl, dy = (i + 1) // 4, (i + 1) % 4
        cp = remote(meta_v.at[t], meta_v.at[t], meta_send.at[i], meta_recv.at[i], d)
        cp.start()
        metas.append((dl, dy))

    def step(k, carry):
        @pl.when(k + 3 < Q)
        def _():
            begin(k + 3)

        @pl.when(k < Q)
        def _():
            arrived(k, 0)
            link(k, got[0], 3, to_p)
            link(k, got[0], 4, to_m)
            sib(k, got[0])

        @pl.when((k >= 2) & (k < Q + 2))
        def _():
            arrived(k - 2, 4)
            link(k - 2, got[4], 6, to_m)
            sib(k - 2, got[4])

        @pl.when(k < Q)
        def _():
            arrived(k, 1)
            link(k, got[1], 5, to_p)
            sib(k, got[1])

        @pl.when((k >= 2) & (k < Q + 2))
        def _():
            for kind in (2, 3, 5):
                arrived(k - 2, kind)
                sib(k - 2, got[kind])

        @pl.when((k >= 3) & (k < Q + 3))
        def _():
            arrived(k - 3, 6)
            sib(k - 3, got[6])

        @pl.when(k == 2)
        def _():
            w_copy.wait()
            for i, (dl, dy) in enumerate(metas):
                source = ((l + dl) % 2) * 4 + (y - dy + 4) % 4
                remote(meta_v.at[source], meta_v.at[source], meta_send.at[i], meta_recv.at[i], to_p).wait()
            to_s = pltpu.make_async_copy(meta_v, meta_s, smem_sem)
            to_s.start()
            to_s.wait()

        @pl.when((k >= 4) & (k < Q + 4))
        def _():
            q = k - 4
            both = feats.at[q, 0:PIECES // 2]
            remote(both, both, link_send.at[7], sib_recv.at[q], to_c).wait_recv()
            for j in range(PAIRS):
                at = slice(j * 2 * HD, (j + 1) * 2 * HD)
                rows = jnp.concatenate([feats[q, p] for p in range(PIECES)], axis=1)
                acc = jnp.dot(rows, w_ref[:, at], preferred_element_type=jnp.float32)
                key = acc[:, :HD]
                layer = (b * PAIRS + j) // KVH
                scale = lax.rsqrt(jnp.mean(key * key, axis=-1, keepdims=True) + norm_eps)
                key = key * scale * gain_ref[pl.ds(layer, 1), :]
                both_kv = jnp.concatenate([key, acc[:, HD:]], axis=1).astype(jnp.bfloat16)
                h_part, r_part = both_kv[:HALF], both_kv[HALF:]
                kv[q, 0, :, at] = h_part
                kv[q, 1, :, at] = r_part
                for dy in range(4):
                    mine = heavy == l * 4 + (y + dy) % 4
                    pay_own[q, dy, :, at] = jnp.where(mine, h_part, r_part)

        @pl.when((k >= 5) & (k < Q + 5))
        def _():
            q = k - 5
            remote(near.at[q], near.at[q], link_send.at[8], near_recv.at[q], to_p).wait_recv()
            near_heavy = meta_s[other, 4, 0]
            h_part, r_part = near[q, 0], near[q, 1]
            for dy in range(4):
                mine = near_heavy == l * 4 + (y + dy) % 4
                pay_near[q, dy] = jnp.where(mine, h_part, r_part)

        @pl.when((k >= 4) & (k < Q + 4))
        def _():
            q = k - 4
            remote(kv.at[q], near.at[q], link_send.at[8], near_recv.at[q], device(h, z, c, 1 - l, y)).start()
            spread(q, pay_own, 0, t)

        @pl.when((k >= 5) & (k < Q + 5))
        def _():
            spread(k - 5, pay_near, 1, other)

        return carry

    lax.fori_loop(0, Q + 5, step, 0)
    meta_out[...] = meta_v[...]

    one = feats.at[:, 0]
    for kind in range(7):
        remote(one, one, link_send.at[kind], link_recv.at[0, kind], to_p).wait_send()
    eight = feats.at[:, 0:PIECES // 2]
    remote(eight, eight, link_send.at[7], sib_recv.at[0], to_c).wait_send()
    remote(kv, near, link_send.at[8], near_recv.at[0], to_p).wait_send()
    for which, pay in ((0, pay_own), (1, pay_near)):
        for dy in (1, 2, 3):
            source = (l if which == 0 else 1 - l) * 4 + (y - dy + 4) % 4
            cp = remote(pay.at[:, dy], cand_ref.at[source], y_send.at[which, dy], y_recv.at[which, dy], to_p)
            cp.wait_send()
            cp.wait_recv()
        pltpu.make_async_copy(pay.at[:, 0], cand_ref.at[t if which == 0 else other], local_sem.at[which]).wait()


def place_kernel(meta_ref, cand_ref, out_ref, took, made, read_sem, write_sem):
    t = lax.axis_index("tile")
    for s in range(8):
        pltpu.make_async_copy(cand_ref.at[s], took.at[s], read_sem.at[s]).start()

    def place(s, carry):
        is_h = (meta_ref[s, 4, 0] == t).astype(jnp.int32)
        pick = [is_h * c for c in range(CAP)]
        used = [is_h] * CAP
        seen = jnp.int32(0)
        for j in range(CAP):
            named = (1 - is_h) * (meta_ref[s, j, 0] == t).astype(jnp.int32)
            for c in range(CAP):
                hit = named * (seen == c).astype(jnp.int32)
                pick[c] = pick[c] + hit * j
                used[c] = used[c] + hit
            seen = seen + named
        pltpu.make_async_copy(cand_ref.at[s], took.at[s], read_sem.at[s]).wait()
        for c in range(CAP):
            block = took[s, pick[c]]
            made[s, c] = jnp.where(used[c] > 0, block, jnp.zeros_like(block))
        pltpu.make_async_copy(made.at[s], out_ref.at[s], write_sem.at[s]).start()
        return carry

    lax.fori_loop(0, 8, place, 0)
    for s in range(8):
        pltpu.make_async_copy(made.at[s], out_ref.at[s], write_sem.at[s]).wait()


def shards(features, weight_kv, key_gain, block_reader):
    dma = pltpu.SemaphoreType.DMA
    bf16 = jnp.bfloat16
    vmem = pl.BlockSpec(memory_space=pltpu.VMEM)
    hbm = pl.BlockSpec(memory_space=pl.ANY)
    cand, meta = pl.pallas_call(
        kv_kernel,
        out_shape=(
            jax.ShapeDtypeStruct((8, Q, HALF, COLS), bf16),
            jax.ShapeDtypeStruct((8, 8, 128), jnp.int32),
        ),
        in_specs=[vmem, hbm, vmem, pl.BlockSpec(memory_space=pltpu.SMEM)],
        out_specs=(hbm, vmem),
        scratch_shapes=[
            pltpu.VMEM((Q, PIECES, ROWS, PIECE), bf16),
            pltpu.VMEM((WIDTH, COLS), bf16),
            pltpu.VMEM((Q, 2, HALF, COLS), bf16),
            pltpu.VMEM((Q, 2, HALF, COLS), bf16),
            pltpu.VMEM((Q, 4, HALF, COLS), bf16),
            pltpu.VMEM((Q, 4, HALF, COLS), bf16),
            pltpu.VMEM((8, 8, 128), jnp.int32),
            pltpu.SMEM((8, 8, 128), jnp.int32),
            dma((9,)),
            dma((Q, 7)),
            dma((Q,)),
            dma((Q,)),
            dma((2, 4)),
            dma((2, 4)),
            dma((7,)),
            dma((7,)),
            dma((2,)),
            dma,
            dma,
        ],
        compiler_params=pltpu.CompilerParams(
            collective_id=0, has_side_effects=True, vmem_limit_bytes=60 * 2**20
        ),
        name="gather_project_route",
    )(features.reshape(BPS * PARTS, HALF, PIECE), weight_kv, key_gain, block_reader)
    slots = pl.pallas_call(
        place_kernel,
        out_shape=jax.ShapeDtypeStruct((8, CAP, BT, COLS), bf16),
        in_specs=[pl.BlockSpec(memory_space=pltpu.SMEM), hbm],
        out_specs=hbm,
        scratch_shapes=[
            pltpu.VMEM((8, CAP, BT, COLS), bf16),
            pltpu.VMEM((8, CAP, BT, COLS), bf16),
            dma((8,)),
            dma((8,)),
        ],
        name="place_slots",
    )(meta, cand.reshape(8, CAP, BT, COLS))
    return slots.reshape(8 * CAP * BT, COLS)


def solution(mesh):
    return jax.shard_map(
        shards,
        mesh=mesh,
        in_specs=(P("tile", "blk"), P(None, "blk"), P(), P("tile")),
        out_specs=P("tile", "blk"),
        check_vma=False,
    )
```
